32 devices in a mesh: wide: 8 (over z, y), narrow: 4 (over x, core).
Axes of the slice: x: 2, y: 2, z: 4, core: 2. Of those that a mesh axis runs over, the one named last changes fastest.
Arguments:
- user_factors: float32 [32768, 512], P(('wide', 'narrow')), may hold values from -1.25 to 1.25
- item_factors: float32 [32, 2, 512, 512], P(('wide', 'narrow')), may hold values from -1.25 to 1.25
- tile_rows: int32 [32, 5, 2, 10], P(('wide', 'narrow')), may hold values from 0 to 7
- tile_cols: int32 [32, 5, 2, 10], P(('wide', 'narrow')), may hold values from 0 to 3
- tile_count: int32 [32, 5, 2], P(('wide', 'narrow')), may hold values from 2 to 10, as said below
- ratings: bfloat16 [32, 5, 2, 10, 128, 128], P(('wide', 'narrow')), may hold values from -6 to 6
Outputs:
- user_result: float32 [32768, 512], P(('wide', 'narrow'))
- item_result: float32 [32, 2, 512, 512], P(('wide', 'narrow'))
The draws below stay inside these ranges and needn't reach their ends.
Inputs may be any that keep to these rules, and one draw needn't show every extreme that they name: At each visit some stratum has 10 tiles in every slot; entries of tile_rows, tile_cols and ratings at minibatch positions tile_count and beyond are not used.
All inputs are finite; a program needn't handle non-finite values.
Results may differ from the reference program's by a relative error of at most 0.0003.
Values sent between devices are 32-bit elements; how exact they have to be, the bound alone decides.
No kernel may reach another device: no remote copies, remote signals or barrier semaphores. Data moves between devices by JAX's collectives and lax.ppermute only.
A program may use at most 64 MiB of HBM per device.

```python
import jax
import jax.numpy as jnp
from jax import lax

RANK = 512
TILE = 128
ITEMS_PER_BLOCK = 512
USER_DEV = 1024
SLOTS = 2
SWEEP_TOTAL = 5
TILES_MOST = 10
CUSTOMER_LAYERS = 32
USERS = 32768
N_WIDE = 8
N_NARROW = 4


def draw_tile_count(key, part):
    shuffle_wave_seed, selected_seed, smaller_submatrix_seed = jax.random.split(key, 3)
    larger_submatrix = jax.random.randint(shuffle_wave_seed, (CUSTOMER_LAYERS, SWEEP_TOTAL, 1), 0, 8) == 0
    chosen = jax.random.randint(selected_seed, (1, SWEEP_TOTAL, 1), 0, CUSTOMER_LAYERS)
    position = jnp.arange(CUSTOMER_LAYERS).reshape(CUSTOMER_LAYERS, 1, 1)
    larger_submatrix = jnp.logical_or(larger_submatrix, position == chosen)
    lighter = jax.random.randint(smaller_submatrix_seed, (CUSTOMER_LAYERS, SWEEP_TOTAL, SLOTS), 2, TILES_MOST // 2 + 1)
    return jnp.where(larger_submatrix, TILES_MOST, lighter).astype(jnp.int32)


def with_ends(drawn, rng, low, high):
    dims = drawn.shape
    place = [jax.random.randint(jax.random.fold_in(rng, axis), (), 0, dims[axis]) for axis in range(len(dims))]
    drawn = drawn.at[tuple(place)].set(low)
    longest = dims.index(max(dims))
    place[longest] = (place[longest] + 1) % dims[longest]
    return drawn.at[tuple(place)].set(high)


def level_of(key, dims, shards, least, high):
    def one(axis_at, blocks):
        steps = jax.random.uniform(jax.random.fold_in(jax.random.fold_in(key, 6), axis_at), (blocks,), jnp.float32, least / len(shards), high / len(shards))
        return jnp.repeat(jnp.exp(steps), dims[axis_at] // blocks).reshape((-1,) + (1,) * (len(dims) - axis_at - 1))

    gain = one(*shards[0])
    for cut in shards[1:]:
        gain = gain * one(*cut)
    return gain


def scatter_about(own_key, shape, width, bound, shards=(), kind=jnp.bfloat16):
    result = width * jax.random.normal(own_key, shape, jnp.float32)
    if shards:
        result = result * level_of(own_key, shape, shards, -0.22, 0.18)
    return jnp.clip(result, -bound, bound).astype(kind)


def setup_inputs(seed: int = 0) -> dict:
    seeds = jax.random.split(jax.random.key(seed), 7)
    return {
        "user_factors": scatter_about(seeds[0], (USERS, RANK), (RANK ** -0.25), 1.25, ((0, 32),), jnp.float32),
        "item_factors": scatter_about(seeds[1], (CUSTOMER_LAYERS, SLOTS, ITEMS_PER_BLOCK, RANK), (RANK ** -0.25), 1.25, ((0, 32),), jnp.float32),
        "tile_rows": with_ends(jax.random.randint(seeds[2], (CUSTOMER_LAYERS, SWEEP_TOTAL, SLOTS, TILES_MOST), 0, USER_DEV // TILE), jax.random.fold_in(seeds[2], 1), 0, (USER_DEV // TILE) - 1).astype(jnp.int32),
        "tile_cols": with_ends(jax.random.randint(seeds[3], (CUSTOMER_LAYERS, SWEEP_TOTAL, SLOTS, TILES_MOST), 0, ITEMS_PER_BLOCK // TILE), jax.random.fold_in(seeds[3], 1), 0, (ITEMS_PER_BLOCK // TILE) - 1).astype(jnp.int32),
        "tile_count": draw_tile_count(jax.random.fold_in(seeds[6], 71), 0),
        "ratings": scatter_about(seeds[5], (CUSTOMER_LAYERS, SWEEP_TOTAL, SLOTS, TILES_MOST, TILE, TILE), 1.0, 6.0, ((0, 32),)),
    }


learn_rate = 0.0035
decay_weight = 0.05


def tile_update(user_block, item_block, rating_tile, row_tile, col_tile):
    tile_size = rating_tile.shape[-1]
    users_part = lax.dynamic_slice_in_dim(user_block, row_tile * tile_size, tile_size, 0)
    items_part = lax.dynamic_slice_in_dim(item_block, col_tile * tile_size, tile_size, 0)
    predicted = lax.dot_general(users_part, items_part, (((1,), (1,)), ((), ())), precision=lax.Precision.HIGHEST, preferred_element_type=jnp.float32)
    errors = predicted - rating_tile.astype(jnp.float32)
    user_grad = jnp.dot(errors, items_part, precision=lax.Precision.HIGHEST, preferred_element_type=jnp.float32) + decay_weight * users_part
    item_gradient = lax.dot_general(errors, users_part, (((0,), (0,)), ((), ())), precision=lax.Precision.HIGHEST, preferred_element_type=jnp.float32) + decay_weight * items_part
    new_users = users_part - learn_rate * user_grad
    new_items = items_part - learn_rate * item_gradient
    user_block = lax.dynamic_update_slice_in_dim(user_block, new_users, row_tile * tile_size, 0)
    item_block = lax.dynamic_update_slice_in_dim(item_block, new_items, col_tile * tile_size, 0)
    return user_block, item_block


def sweep_slot(user_block, item_block, ratings_slot, rows_slot, cols_slot, tile_total):
    def one_tile(position, carried):
        user_now, item_now = carried
        return tile_update(user_now, item_now, ratings_slot[position], rows_slot[position], cols_slot[position])

    return lax.fori_loop(0, tile_total, one_tile, (user_block, item_block))


def reference(user_factors, item_factors, tile_rows, tile_cols, tile_count, ratings):
    user_blocks = user_factors.reshape(CUSTOMER_LAYERS, USER_DEV, RANK)
    held_blocks = item_factors
    for visit_index in range(SWEEP_TOTAL):
        if visit_index > 0:
            layout_grid = held_blocks.reshape(N_WIDE, N_NARROW, SLOTS, ITEMS_PER_BLOCK, RANK)
            layout_grid = jnp.roll(layout_grid, 1, axis=0)
            if visit_index == SWEEP_TOTAL - 1:
                layout_grid = jnp.roll(layout_grid, 1, axis=1)
            held_blocks = layout_grid.reshape(CUSTOMER_LAYERS, SLOTS, ITEMS_PER_BLOCK, RANK)
        new_slots = []
        for holder_position in range(SLOTS):
            user_blocks, holder_product_factors = jax.vmap(sweep_slot)(
                user_blocks,
                held_blocks[:, holder_position],
                ratings[:, visit_index, holder_position],
                tile_rows[:, visit_index, holder_position],
                tile_cols[:, visit_index, holder_position],
                tile_count[:, visit_index, holder_position],
            )
            new_slots.append(holder_product_factors)
        held_blocks = jnp.stack(new_slots, axis=1)
    return (user_blocks.reshape(USERS, RANK), held_blocks)
```

```python
import jax
import jax.numpy as jnp
from jax import lax
from jax.experimental import pallas as pl
from jax.experimental.pallas import tpu as pltpu
from jax.sharding import PartitionSpec as P

learn_rate = 0.0035
decay_weight = 0.05


def split(value):
    high = value.astype(jnp.bfloat16)
    low = (value - high.astype(jnp.float32)).astype(jnp.bfloat16)
    return high, low


def product(left, right, dims):
    return lax.dot_general(left, right, (dims, ((), ())), preferred_element_type=jnp.float32)


def sweep_kernel(visit, slot, rows, cols, count, user_in, item_in, ratings, user_out, item_out):
    tile = ratings.shape[-1]
    user_out[...] = user_in[...]
    item_out[...] = item_in[...]

    def one_tile(k, carry):
        a = pl.multiple_of(rows[0, visit, slot, k] * tile, tile)
        c = pl.multiple_of(cols[0, visit, slot, k] * tile, tile)
        users = user_out[pl.ds(a, tile), :]
        items = item_out[pl.ds(c, tile), :]
        users_cat = jnp.concatenate(split(users), 0)
        items_cat = jnp.concatenate(split(items), 0)
        quads = product(users_cat, items_cat, ((1,), (1,)))
        predicted = (quads[:tile, :tile] + (quads[:tile, tile:] + quads[tile:, :tile])) + quads[tile:, tile:]
        errors = predicted - ratings[0, 0, 0, k].astype(jnp.float32)
        high, low = split(errors)
        high_t, low_t = split(errors.T)
        errors_cat = jnp.concatenate([jnp.concatenate([high, high], 1), jnp.concatenate([low, low], 1)], 0)
        errors_t_cat = jnp.concatenate([jnp.concatenate([high_t, high_t], 1), jnp.concatenate([low_t, low_t], 1)], 0)
        user_grad = product(errors_cat, items_cat, ((1,), (0,)))
        item_grad = product(errors_t_cat, users_cat, ((1,), (0,)))
        user_grad = user_grad[:tile] + user_grad[tile:] + decay_weight * users
        item_grad = item_grad[:tile] + item_grad[tile:] + decay_weight * items
        user_out[pl.ds(a, tile), :] = users - learn_rate * user_grad
        item_out[pl.ds(c, tile), :] = items - learn_rate * item_grad
        return carry

    lax.fori_loop(0, count[0, visit, slot], one_tile, 0)


def sweep_slot(visit, slot, rows, cols, count, user_block, item_block, ratings):
    def kernel(*refs):
        sweep_kernel(visit, slot, *refs)

    scalars = pl.BlockSpec(memory_space=pltpu.SMEM)
    whole = pl.BlockSpec(memory_space=pltpu.VMEM)
    block = (1, 1, 1) + ratings.shape[3:]
    return pl.pallas_call(
        kernel,
        grid=(1,),
        in_specs=[scalars, scalars, scalars, whole, whole,
                  pl.BlockSpec(block, lambda i: (0, visit, slot, 0, 0, 0))],
        out_specs=[whole, whole],
        out_shape=[jax.ShapeDtypeStruct(user_block.shape, user_block.dtype),
                   jax.ShapeDtypeStruct(item_block.shape, item_block.dtype)],
        input_output_aliases={3: 0, 4: 1},
        name=f"sweep_{visit}_{slot}",
    )(rows, cols, count, user_block, item_block, ratings)


def body(user_factors, item_factors, tile_rows, tile_cols, tile_count, ratings):
    axes = ("wide", "narrow")
    wide, narrow = lax.axis_size("wide"), lax.axis_size("narrow")
    visits = ratings.shape[1]
    slots = ratings.shape[2]

    def shifted(block, by_wide, by_narrow):
        route = [(w * narrow + n, (w + by_wide) % wide * narrow + (n + by_narrow) % narrow)
                 for w in range(wide) for n in range(narrow)]
        return lax.ppermute(block, axes, route)

    user_block = user_factors
    held = [item_factors[0, s] for s in range(slots)]
    for v in range(visits):
        for s in range(slots):
            user_block, held[s] = sweep_slot(v, s, tile_rows, tile_cols, tile_count, user_block, held[s], ratings)
            if v < visits - 1:
                held[s] = shifted(held[s], 1, 1 if v == visits - 2 else 0)
    return user_block, jnp.stack(held, 0)[None]


def solution(mesh):
    in_specs = (
        P(("wide", "narrow"), None),
        P(("wide", "narrow"), None, None, None),
        P(("wide", "narrow"), None, None, None),
        P(("wide", "narrow"), None, None, None),
        P(("wide", "narrow"), None, None),
        P(("wide", "narrow"), None, None, None, None, None),
    )
    out_specs = (P(("wide", "narrow"), None), P(("wide", "narrow"), None, None, None))
    return jax.shard_map(body, mesh=mesh, in_specs=in_specs, out_specs=out_specs, check_vma=False)
```
